32 devices in a mesh: freq: 16 (over z, y, x), plane: 2 (over core).
Axes of the slice: x: 2, y: 2, z: 4, core: 2. Of those that a mesh axis runs over, the one named last changes fastest.
Arguments:
- state_in: float32 [2, 32, 5, 256, 128], P(None, 'freq', None, 'plane'), may hold values from -6 to 6
- forcing_in: float32 [2, 32, 5, 256, 128], P(None, 'freq', None, 'plane'), may hold values from -6 to 6
- base_flow: float32 [16, 5, 256, 128], P('freq', None, 'plane'), may hold values from -1 to 1
- station_index: int32 [2], replicated, may hold values from 0 to 15
- lobe_count: int32 [1], replicated, may hold values from 3 to 127
Outputs:
- state_out: float32 [2, 32, 5, 256, 128], P(None, 'freq', None, 'plane')
- forcing_out: float32 [2, 32, 5, 256, 128], P(None, 'freq', None, 'plane')
The draws below stay inside these ranges and needn't reach their ends.
All inputs are finite; a program needn't handle non-finite values.
Results may differ from the reference program's by a relative error of at most 0.0003.
Values sent between devices are 32-bit elements; how exact they have to be, the bound alone decides.
A program may use at most 128 MiB of HBM per device.

```python
import math
import jax
import jax.numpy as jnp
from jax import lax

VARS = 5
R = 128
A = 256
SWEEPS = 4
STEPS = 2
F = 32
NT = 48
STATIONS = 16


def block_levels(stream_key, dims, split, smallest, largest):
    gain, own = 1.0, jax.random.fold_in(stream_key, 6)
    for dim, parts in split:
        heights = jnp.exp(jax.random.uniform(jax.random.fold_in(own, dim), (parts,), jnp.float32, smallest / len(split), largest / len(split)))
        gain = gain * jnp.repeat(heights, dims[dim] // parts).reshape([-1 if axis == dim else 1 for axis in range(len(dims))])
    return gain


def noise(own_key, dims, scale, bound, shards=(), held_as=jnp.bfloat16):
    array = jax.random.normal(own_key, dims, jnp.float32) * scale
    if len(shards) > 0:
        array = block_levels(own_key, dims, shards, -0.22, 0.18) * array
    return jnp.clip(array, min=-bound, max=bound).astype(held_as)


def setup_inputs(seed: int = 0) -> dict:
    streams_of = jax.random.split(jax.random.key(seed), 6)
    state_in = noise(streams_of[0], (2, F, VARS, A, R), 1.0, 6.0, ((1, 16), (3, 2)), jnp.float32)
    forcing_in = noise(streams_of[1], (2, F, VARS, A, R), 1.0, 6.0, ((1, 16), (3, 2)), jnp.float32)
    base_flow = jnp.clip(jax.random.uniform(streams_of[2], (STATIONS, VARS, A, R), jnp.float32, -1.0, 1.0) * block_levels(streams_of[2], (STATIONS, VARS, A, R), ((0, 16), (2, 2)), -0.4, 0.0), -1.0, 1.0)
    station_index = jax.random.randint(streams_of[3], (STEPS,), 0, STATIONS).astype(jnp.int32)
    lobe_count = jax.random.randint(streams_of[4], (1,), 3, 128).astype(jnp.int32)
    return {"state_in": state_in, "forcing_in": forcing_in, "base_flow": base_flow, "station_index": station_index, "lobe_count": lobe_count}


SIDE_WEIGHT = 1.25
MARCH_WEIGHT = 4.0
DIAG_SHIFT = 4.0
ADVECT_SCALE = 0.5
BASE_SCALE = 0.5
HIGHEST_MODE = lax.Precision.HIGHEST

def radial_tables(radius_count):
    indices = jnp.arange(radius_count)
    angles = math.pi * indices.astype(jnp.float32) / (radius_count - 1)
    cheb_nodes = jnp.cos(angles)
    weights = jnp.where((indices == 0) | (indices == radius_count - 1), 2.0, 1.0).astype(jnp.float32)
    parity = (1 - 2 * ((indices[:, None] + indices[None, :]) % 2)).astype(jnp.float32)
    offdiag = indices[:, None] != indices[None, :]
    spacing = jnp.where(offdiag, cheb_nodes[:, None] - cheb_nodes[None, :], 1.0)
    entries = jnp.where(offdiag, weights[:, None] / weights[None, :] * parity / spacing, 0.0)
    entries = entries - jnp.diag(lax.optimization_barrier(jnp.sum(entries, axis=1)))
    slopes = jnp.sin(angles)[:, None] * entries / (radius_count - 1)
    stiffness = jnp.dot(slopes.T, slopes, precision=HIGHEST_MODE)
    system = stiffness + DIAG_SHIFT * jnp.eye(radius_count, dtype=jnp.float32)
    factor = jnp.linalg.cholesky(system)
    factor_inv = lax.linalg.triangular_solve(factor, jnp.eye(radius_count, dtype=jnp.float32), left_side=True, lower=True)
    return (slopes, jnp.dot(factor_inv.T, factor_inv, precision=HIGHEST_MODE))

def transform_tables(freqs, ntime):
    mode_ids = jnp.arange(freqs)
    time_ids = jnp.arange(ntime)
    phases = mode_ids[:, None] * time_ids[None, :] % ntime
    angles = 2.0 * math.pi * phases.astype(jnp.float32) / ntime
    cosines = jnp.cos(angles)
    sine_tab = jnp.sin(angles)
    stacked = jnp.concatenate([cosines, -sine_tab], axis=0)
    return (stacked.T / math.sqrt(freqs), stacked / math.sqrt(ntime))

def chevron(lobe_count, azimuths, start_az, total_az):
    position = (start_az + jnp.arange(azimuths)).astype(jnp.int32)
    phases = lobe_count[0] * position % total_az
    return 1.0 + 0.5 * jnp.cos(2.0 * math.pi * phases.astype(jnp.float32) / total_az)

def relax_sweep(inner, neighbours, right_side, coefficient, omegas, inverse_p):
    real_part = inner[0]
    imag_part = inner[1]
    rate_col = omegas[:, None, None, None]
    scaled = coefficient[None]
    mixing = jnp.stack([scaled * real_part - rate_col * imag_part, scaled * imag_part + rate_col * real_part])
    summed = right_side - mixing + SIDE_WEIGHT * neighbours
    radius_count = summed.shape[-1]
    return jnp.dot(summed.reshape(-1, radius_count), inverse_p.T, precision=HIGHEST_MODE).reshape(summed.shape)

def advect(velocity, radial_time, around_time):
    carried = velocity[:, 1:2] * radial_time + velocity[:, 2:3] * around_time
    spread = velocity[:, 0] * (radial_time[:, 1] + around_time[:, 2])
    carried = jnp.concatenate([carried[:, 0:1] + spread[:, None], carried[:, 1:]], axis=1)
    return -ADVECT_SCALE * carried

def forcing_of(march_state, slopes, inverse, forward):
    radial = jnp.dot(march_state.reshape(-1, R), slopes.T, precision=HIGHEST_MODE).reshape(march_state.shape)
    beside_all = 0.5 * (jnp.roll(march_state, -1, 3) - jnp.roll(march_state, 1, 3))
    fields = jnp.stack([march_state, radial, beside_all])
    az_block = 32 if A % 32 == 0 else A
    pieces = []
    for first_az in range(0, A, az_block):
        block_data = fields[:, :, :, :, first_az:first_az + az_block, :].reshape(3, 2 * F, -1)
        in_time = jnp.einsum('tc,kcx->ktx', inverse, block_data, precision=HIGHEST_MODE).reshape(3, NT, VARS, -1)
        source = advect(in_time[0], in_time[1], in_time[2])
        spectral = jnp.dot(forward, source.reshape(NT, -1), precision=HIGHEST_MODE)
        pieces.append(spectral.reshape(2, F, VARS, az_block, R))
    return jnp.concatenate(pieces, axis=3)

def reference(state_in, forcing_in, base_flow, station_index, lobe_count):
    slopes, inverse_p = radial_tables(R)
    inverse, forward = transform_tables(F, NT)
    omegas = 0.5 * jnp.arange(F).astype(jnp.float32) / F
    shape_az = chevron(lobe_count, A, 0, A)
    march_state = state_in
    forcing = forcing_in
    for station in range(STEPS):
        plane_flow = lax.dynamic_index_in_dim(base_flow, station_index[station], 0, keepdims=False)
        coefficient = BASE_SCALE * plane_flow * shape_az[None, :, None]
        right_side = MARCH_WEIGHT * march_state + forcing
        iterate = march_state
        for sweep_no in range(SWEEPS):
            iterate = relax_sweep(iterate, jnp.roll(iterate, -1, 3) + jnp.roll(iterate, 1, 3), right_side, coefficient, omegas, inverse_p)
        march_state = iterate
        forcing = forcing_of(march_state, slopes, inverse, forward)
    return (march_state, forcing)
```

```python
import math

import jax
import jax.numpy as jnp
import numpy as np
from jax import lax
from jax.sharding import PartitionSpec as P

SWEEPS = 4
STEPS = 2


SIDE_WEIGHT = 1.25
MARCH_WEIGHT = 4.0
DIAG_SHIFT = 4.0
ADVECT_SCALE = 0.5
BASE_SCALE = 0.5
HIGHEST_MODE = lax.Precision.HIGHEST


def radial_tables(radius_count):
    indices = np.arange(radius_count)
    angles = math.pi * indices / (radius_count - 1)
    nodes = np.cos(angles)
    weights = np.where((indices == 0) | (indices == radius_count - 1), 2.0, 1.0)
    parity = 1.0 - 2.0 * ((indices[:, None] + indices[None, :]) % 2)
    offdiag = indices[:, None] != indices[None, :]
    spacing = np.where(offdiag, nodes[:, None] - nodes[None, :], 1.0)
    entries = np.where(offdiag, weights[:, None] / weights[None, :] * parity / spacing, 0.0)
    entries = entries - np.diag(entries.sum(axis=1))
    slopes = np.sin(angles)[:, None] * entries / (radius_count - 1)
    system = slopes.T @ slopes + DIAG_SHIFT * np.eye(radius_count)
    return slopes.astype(np.float32), np.linalg.inv(system).astype(np.float32)


def transform_tables(mode_ids, freqs, ntime):
    time_ids = np.arange(ntime)
    angles = 2.0 * math.pi * (mode_ids[:, None] * time_ids[None, :] % ntime) / ntime
    stacked = np.stack([np.cos(angles), -np.sin(angles)])
    return (
        (stacked / math.sqrt(freqs)).astype(np.float32),
        (stacked / math.sqrt(ntime)).astype(np.float32),
    )


def chevron(lobe_count, azimuths, start_az, total_az):
    position = start_az + jnp.arange(azimuths)
    phases = lobe_count[0] * position % total_az
    return 1.0 + 0.5 * jnp.cos(2.0 * math.pi * phases.astype(jnp.float32) / total_az)


def per_device(state_in, forcing_in, base_flow, station_index, lobe_count):
    _, per_dev, variables, span_az, radius_count = state_in.shape
    nf = lax.axis_size("freq")
    planes = lax.axis_size("plane")
    freqs = per_dev * nf
    ntime = 3 * freqs // 2
    own_az = span_az // nf
    slopes, inverse_p = radial_tables(radius_count)
    mode_ids = (np.arange(nf)[None, :] * per_dev + np.arange(per_dev)[:, None]).reshape(-1)
    inverse, forward = transform_tables(mode_ids, freqs, ntime)
    omegas = (0.5 * mode_ids / freqs).astype(np.float32)[:, None]
    f = lax.axis_index("freq")
    shape_az = chevron(
        lobe_count,
        own_az,
        lax.axis_index("plane") * span_az + f * own_az,
        span_az * planes,
    )
    ring = nf * planes
    order = [f_at * planes + p_at for p_at in range(planes) for f_at in range(nf)]
    up = [(order[i], order[(i + 1) % ring]) for i in range(ring)]
    down = [(b, a) for a, b in up]

    def edges(x):
        before = lax.ppermute(x[-1:], ("freq", "plane"), up)
        after = lax.ppermute(x[:1], ("freq", "plane"), down)
        return before, after

    def to_chunks(x):
        x = x.reshape(2, per_dev, variables, nf, own_az, radius_count)
        return x.transpose(3, 4, 0, 2, 1, 5)

    stored = base_flow.shape[0]
    planes_out = base_flow.reshape(stored, variables, nf, own_az, radius_count)
    planes_all = lax.all_to_all(
        planes_out.transpose(2, 0, 3, 1, 4), "freq", split_axis=0, concat_axis=0, tiled=True
    ).reshape(nf * stored, own_az, variables, radius_count)
    fields = jnp.stack([to_chunks(state_in), to_chunks(forcing_in)], axis=1)
    fields = lax.all_to_all(fields, "freq", split_axis=0, concat_axis=0, tiled=True)
    fields = fields.transpose(1, 2, 3, 4, 5, 0, 6).reshape(
        2, own_az, 2, variables, freqs, radius_count
    )
    state, forcing = fields[0], fields[1]
    for station in range(STEPS):
        plane_flow = lax.dynamic_index_in_dim(planes_all, station_index[station], 0, keepdims=False)
        coefficient = (BASE_SCALE * plane_flow * shape_az[:, None, None])[:, :, None, :]
        right_side = MARCH_WEIGHT * state + forcing
        for sweep_no in range(SWEEPS):
            before, after = edges(state)
            around = jnp.concatenate([before, state[:-1]]) + jnp.concatenate([state[1:], after])
            real, imag = state[:, 0], state[:, 1]
            mixing = jnp.stack(
                [coefficient * real - omegas * imag, coefficient * imag + omegas * real], axis=1
            )
            summed = right_side - mixing + SIDE_WEIGHT * around
            state = jnp.dot(
                summed.reshape(-1, radius_count), inverse_p.T, precision=HIGHEST_MODE
            ).reshape(summed.shape)
        before, after = edges(state)
        beside = 0.5 * (jnp.concatenate([state[1:], after]) - jnp.concatenate([before, state[:-1]]))
        both = jnp.stack([state, beside])
        in_time = jnp.einsum("ckt,facvkr->fatvr", inverse, both, precision=HIGHEST_MODE)
        velocity, around_time = in_time[0], in_time[1]
        radial_time = jnp.dot(
            velocity.reshape(-1, radius_count), slopes.T, precision=HIGHEST_MODE
        ).reshape(velocity.shape)
        carried = velocity[:, :, 1:2] * radial_time + velocity[:, :, 2:3] * around_time
        spread = velocity[:, :, 0:1] * (radial_time[:, :, 1:2] + around_time[:, :, 2:3])
        carried = jnp.concatenate([carried[:, :, 0:1] + spread, carried[:, :, 1:]], axis=2)
        source = -ADVECT_SCALE * carried
        forcing = jnp.einsum("ckt,atvr->acvkr", forward, source, precision=HIGHEST_MODE)
    outs = jnp.stack([state, forcing]).reshape(
        2, own_az, 2, variables, per_dev, nf, radius_count
    )
    outs = lax.all_to_all(
        outs.transpose(5, 0, 1, 2, 3, 4, 6), "freq", split_axis=0, concat_axis=0, tiled=True
    )
    outs = outs.transpose(1, 3, 5, 4, 0, 2, 6).reshape(
        2, 2, per_dev, variables, span_az, radius_count
    )
    return outs[0], outs[1]


def solution(mesh):
    return jax.shard_map(
        per_device,
        mesh=mesh,
        in_specs=(
            P(None, "freq", None, "plane", None),
            P(None, "freq", None, "plane", None),
            P("freq", None, "plane", None),
            P(),
            P(),
        ),
        out_specs=(P(None, "freq", None, "plane", None), P(None, "freq", None, "plane", None)),
        check_vma=False,
    )
```

```python
import functools
import math

import jax
import jax.numpy as jnp
import numpy as np
from jax import lax
from jax.experimental import pallas as pl
from jax.experimental.pallas import tpu as pltpu
from jax.sharding import PartitionSpec as P

SWEEPS = 4
STEPS = 2


SIDE_WEIGHT = 1.25
MARCH_WEIGHT = 4.0
DIAG_SHIFT = 4.0
ADVECT_SCALE = 0.5
BASE_SCALE = 0.5
HIGHEST_MODE = lax.Precision.HIGHEST


def radial_tables(radius_count):
    indices = np.arange(radius_count)
    angles = math.pi * indices / (radius_count - 1)
    nodes = np.cos(angles)
    weights = np.where((indices == 0) | (indices == radius_count - 1), 2.0, 1.0)
    parity = 1.0 - 2.0 * ((indices[:, None] + indices[None, :]) % 2)
    offdiag = indices[:, None] != indices[None, :]
    spacing = np.where(offdiag, nodes[:, None] - nodes[None, :], 1.0)
    entries = np.where(offdiag, weights[:, None] / weights[None, :] * parity / spacing, 0.0)
    entries = entries - np.diag(entries.sum(axis=1))
    slopes = np.sin(angles)[:, None] * entries / (radius_count - 1)
    system = slopes.T @ slopes + DIAG_SHIFT * np.eye(radius_count)
    return slopes.astype(np.float32), np.linalg.inv(system).astype(np.float32)


def transform_tables(mode_ids, freqs, ntime):
    time_ids = np.arange(ntime)
    angles = 2.0 * math.pi * (mode_ids[:, None] * time_ids[None, :] % ntime) / ntime
    stacked = np.stack([np.cos(angles), -np.sin(angles)])
    return (
        (stacked / math.sqrt(freqs)).astype(np.float32),
        (stacked / math.sqrt(ntime)).astype(np.float32),
    )


def chevron(lobe_count, azimuths, start_az, total_az):
    position = start_az + jnp.arange(azimuths)
    phases = lobe_count[0] * position % total_az
    return 1.0 + 0.5 * jnp.cos(2.0 * math.pi * phases.astype(jnp.float32) / total_az)


def block_of(f, p, nf):
    j = f
    if nf % 4 == 0:
        z, y, x = f // 4, (f // 2) % 2, f % 2
        r = 2 * y + (x + y) % 2
        j = 4 * z + r + (z % 2) * (3 - 2 * r)
    return j + (p % 2) * (nf - 1 - 2 * j)


def freq_of(block, p, nf):
    j = block + (p % 2) * (nf - 1 - 2 * block)
    if nf % 4 == 0:
        z, r = j // 4, j % 4
        r = r + (z % 2) * (3 - 2 * r)
        y = r // 2
        return 4 * z + 2 * y + (r + y) % 2
    return j


def march(
    dims,
    station_ref,
    shape_ref,
    s_state,
    s_base,
    s_forcing,
    omega_ref,
    qt_ref,
    st_ref,
    inv_ref,
    fwd_ref,
    g_state,
    g_forcing,
    r_state,
    r_base,
    r_forcing,
    x_ref,
    b_ref,
    f_ref,
    w_ref,
    o_state,
    o_forcing,
    send_sem,
    recv_sem,
    own_sem,
    halo_send,
    halo_recv,
):
    nf, planes, own_az, variables, per_dev, radii, stored, rows, base_rows = dims
    freqs = nf * per_dev
    ntime = inv_ref.shape[0]
    half = variables * freqs
    me = lax.axis_index("freq")
    plane = lax.axis_index("plane")
    block = block_of(me, plane, nf)
    ring = nf * planes
    here = plane * nf + block
    right, left = (here + 1) % ring, (here + ring - 1) % ring

    def at_ring(g):
        p = g // nf
        return {"freq": freq_of(g % nf, p, nf), "plane": p}

    right_id, left_id = at_ring(right), at_ring(left)

    barrier = pltpu.get_barrier_semaphore()

    @pl.loop(1, nf)
    def _(d):
        pl.semaphore_signal(
            barrier, inc=1, device_id={"freq": (me + d) % nf, "plane": plane}, device_id_type=MESH
        )

    for target in (right_id, left_id):
        pl.semaphore_signal(barrier, inc=1, device_id=target, device_id_type=MESH)
    pl.semaphore_wait(barrier, nf + 1)

    def exchange(k, source, landing, index_to, mine, size, first):
        def copy(d):
            other = (me + d) % nf
            src = source.at[pl.ds(pl.multiple_of(index_to(other) * size, 8), size), :]
            dst = landing.at[pl.ds(pl.multiple_of(mine * size, 8), size), :]
            return pltpu.make_async_remote_copy(
                src_ref=src,
                dst_ref=dst,
                send_sem=send_sem.at[k, d],
                recv_sem=recv_sem.at[k, d],
                device_id={"freq": other, "plane": plane},
                device_id_type=MESH,
            )

        own = pltpu.make_async_copy(
            source.at[pl.ds(pl.multiple_of(index_to(me) * size, 8), size), :],
            landing.at[pl.ds(pl.multiple_of(mine * size, 8), size), :],
            own_sem.at[k],
        )
        if first:

            @pl.loop(1, nf)
            def _(d):
                copy(d).start()

            own.start()
        else:

            @pl.loop(1, nf)
            def _(d):
                copy(d).wait()

            own.wait()

    def to_block(f):
        return block_of(f, plane, nf)

    def to_freq(f):
        return f

    base_args = (1, s_base, r_base, to_block, me, base_rows)
    state_args = (0, s_state, r_state, to_block, me, rows)
    forcing_args = (2, s_forcing, r_forcing, to_block, me, rows)
    out_state_args = (3, o_state, g_state, to_freq, block, rows)
    out_forcing_args = (4, o_forcing, g_forcing, to_freq, block, rows)
    for args in (state_args, base_args, forcing_args):
        exchange(*args, True)

    def halo_copies(e):
        slot = e % 2
        return (
            pltpu.make_async_remote_copy(
                src_ref=x_ref.at[slot, own_az],
                dst_ref=x_ref.at[slot, 0],
                send_sem=halo_send.at[0, e],
                recv_sem=halo_recv.at[0, e],
                device_id=right_id,
                device_id_type=MESH,
            ),
            pltpu.make_async_remote_copy(
                src_ref=x_ref.at[slot, 1],
                dst_ref=x_ref.at[slot, own_az + 1],
                send_sem=halo_send.at[1, e],
                recv_sem=halo_recv.at[1, e],
                device_id=left_id,
                device_id_type=MESH,
            ),
        )

    def place(a, c, v, kk):
        return ((c * variables + v) * per_dev + kk) * nf

    def packed_row(a, c, v, kk):
        return ((c * per_dev + kk) * variables + v) * own_az + a

    def each_run(visit):
        @pl.loop(0, own_az)
        def _(a):
            for c in range(2):
                for v in range(variables):
                    for kk in range(per_dev):
                        visit(a, place(a, c, v, kk), packed_row(a, c, v, kk))

    exchange(*state_args, False)

    def unpack_state(a, start, row):
        x_ref[0, a + 1, pl.ds(start, nf), :] = r_state[pl.ds(row, nf, stride=rows), :]

    each_run(unpack_state)
    for copy in halo_copies(0):
        copy.start()
    exchange(*base_args, False)
    exchange(*forcing_args, False)

    def unpack_forcing(a, start, row):
        b_ref[a, pl.ds(start, nf), :] = (
            MARCH_WEIGHT * x_ref[0, a + 1, pl.ds(start, nf), :]
            + r_forcing[pl.ds(row, nf, stride=rows), :]
        )

    each_run(unpack_forcing)
    omega = omega_ref[...][None]
    flat = (2 * half, radii)
    cube = (variables, freqs, radii)

    def sweep_slab(src, dst, a):
        x = x_ref[src, a + 1]
        beside = SIDE_WEIGHT * (x_ref[src, a] + x_ref[src, a + 2]) + b_ref[a]
        real, imag = x[:half].reshape(cube), x[half:].reshape(cube)
        w = w_ref[a][:variables][:, None, :]
        mixing = jnp.concatenate([w * real - omega * imag, w * imag + omega * real], axis=0)
        summed = beside - mixing.reshape(flat)
        x_ref[dst, a + 1] = jnp.dot(
            summed, qt_ref[...], precision=HIGHEST_MODE, preferred_element_type=jnp.float32
        )

    def advect_slab(slot, a, final):
        x = x_ref[slot, a + 1]
        beside = 0.5 * (x_ref[slot, a + 2] - x_ref[slot, a])

        def lanes(y):
            return [
                jnp.concatenate(
                    [
                        y[v * freqs : (v + 1) * freqs],
                        y[half + v * freqs : half + (v + 1) * freqs],
                    ],
                    axis=0,
                )
                for v in range(variables)
            ]

        both = jnp.concatenate(lanes(x) + lanes(beside), axis=1)
        in_time = jnp.dot(
            inv_ref[...], both, precision=HIGHEST_MODE, preferred_element_type=jnp.float32
        )
        u = [in_time[:, v * radii : (v + 1) * radii] for v in range(variables)]
        ua = [
            in_time[:, (variables + v) * radii : (variables + v + 1) * radii]
            for v in range(variables)
        ]
        radial = jnp.dot(
            jnp.concatenate(u, axis=0),
            st_ref[...],
            precision=HIGHEST_MODE,
            preferred_element_type=jnp.float32,
        )
        ur = [radial[v * ntime : (v + 1) * ntime] for v in range(variables)]
        n = [u[1] * ur[v] + u[2] * ua[v] for v in range(variables)]
        n[0] = n[0] + u[0] * (ur[1] + ua[2])
        source = -ADVECT_SCALE * jnp.concatenate(n, axis=1)
        spectral = jnp.dot(
            fwd_ref[...], source, precision=HIGHEST_MODE, preferred_element_type=jnp.float32
        )
        forcing = jnp.concatenate(
            [
                spectral[c * freqs : (c + 1) * freqs, v * radii : (v + 1) * radii]
                for c in range(2)
                for v in range(variables)
            ],
            axis=0,
        )
        if final:
            f_ref[a] = forcing
        else:
            b_ref[a] = MARCH_WEIGHT * x + forcing

    for station in range(STEPS):
        wanted = station_ref[station]

        @pl.loop(0, own_az)
        def _(a):
            for v in range(variables):
                w_ref[a, pl.ds(v, 1), :] = (BASE_SCALE * shape_ref[a]) * r_base[
                    pl.ds(
                        (wanted // stored) * base_rows
                        + ((wanted % stored) * variables + v) * own_az
                        + a,
                        1,
                    ),
                    :,
                ]

        @pl.loop(0, SWEEPS)
        def _(sweep):
            e = station * SWEEPS + sweep
            src, dst = e % 2, (e + 1) % 2

            @pl.when((sweep > 0) | (station == 0))
            def _():
                for copy in halo_copies(e):
                    copy.wait()

            sweep_slab(src, dst, 0)
            if own_az > 1:
                sweep_slab(src, dst, own_az - 1)
            for copy in halo_copies(e + 1):
                copy.start()

            @pl.loop(1, own_az - 1)
            def _(a):
                sweep_slab(src, dst, a)

        last = (station + 1) * SWEEPS
        slot = last % 2
        final = station == STEPS - 1
        if final:

            def pack_state(a, start, row):
                o_state[pl.ds(row, nf, stride=rows), :] = x_ref[slot, a + 1, pl.ds(start, nf), :]

            each_run(pack_state)
            exchange(*out_state_args, True)

        @pl.loop(1, own_az - 1)
        def _(a):
            advect_slab(slot, a, final)

        for copy in halo_copies(last):
            copy.wait()
        advect_slab(slot, 0, final)
        if own_az > 1:
            advect_slab(slot, own_az - 1, final)

    def pack_forcing(a, start, row):
        o_forcing[pl.ds(row, nf, stride=rows), :] = f_ref[a, pl.ds(start, nf), :]

    each_run(pack_forcing)
    exchange(*out_forcing_args, True)
    exchange(*out_state_args, False)
    exchange(*out_forcing_args, False)


def per_device(state_in, forcing_in, base_flow, station_index, lobe_count):
    _, per_dev, variables, span_az, radii = state_in.shape
    nf = lax.axis_size("freq")
    planes = lax.axis_size("plane")
    freqs = per_dev * nf
    ntime = 3 * freqs // 2
    own_az = span_az // nf
    stored = base_flow.shape[0]
    slopes, inverse_p = radial_tables(radii)
    mode_ids = (np.arange(nf)[None, :] * per_dev + np.arange(per_dev)[:, None]).reshape(-1)
    inverse, forward = transform_tables(mode_ids, freqs, ntime)
    omegas = np.broadcast_to((0.5 * mode_ids / freqs).astype(np.float32)[:, None], (freqs, radii))
    plane = lax.axis_index("plane")
    block = block_of(lax.axis_index("freq"), plane, nf)
    shape_az = chevron(lobe_count, own_az, plane * span_az + block * own_az, span_az * planes)

    def padded_rows(count):
        return -(-count // 8) * 8

    def chunks(x, size):
        x = x.reshape(-1, nf, own_az, radii).transpose(1, 0, 2, 3).reshape(nf, -1, radii)
        x = jnp.pad(x, ((0, 0), (0, size - x.shape[1]), (0, 0)))
        return x.reshape(nf * size, radii)

    count = 2 * per_dev * variables * own_az
    rows = padded_rows(count)
    base_rows = padded_rows(stored * variables * own_az)
    dims = (nf, planes, own_az, variables, per_dev, radii, stored, rows, base_rows)
    half = variables * freqs
    exchanges = STEPS * SWEEPS + 1
    vmem = pl.BlockSpec(memory_space=pltpu.VMEM)
    smem = pl.BlockSpec(memory_space=pltpu.SMEM)
    anywhere = pl.BlockSpec(memory_space=pl.ANY)
    packed = (nf * rows, radii)
    f32 = jnp.float32
    outs = pl.pallas_call(
        functools.partial(march, dims),
        out_shape=[jax.ShapeDtypeStruct(packed, f32)] * 2,
        in_specs=[smem, smem, anywhere, anywhere, anywhere] + [vmem] * 5,
        out_specs=[anywhere, anywhere],
        scratch_shapes=[
            pltpu.VMEM(packed, f32),
            pltpu.VMEM((nf * base_rows, radii), f32),
            pltpu.VMEM(packed, f32),
            pltpu.VMEM((2, own_az + 2, 2 * half, radii), f32),
            pltpu.VMEM((own_az, 2 * half, radii), f32),
            pltpu.VMEM((own_az, 2 * half, radii), f32),
            pltpu.VMEM((own_az, padded_rows(variables), radii), f32),
            pltpu.VMEM(packed, f32),
            pltpu.VMEM(packed, f32),
            pltpu.SemaphoreType.DMA((5, nf)),
            pltpu.SemaphoreType.DMA((5, nf)),
            pltpu.SemaphoreType.DMA((5,)),
            pltpu.SemaphoreType.DMA((2, exchanges)),
            pltpu.SemaphoreType.DMA((2, exchanges)),
        ],
        compiler_params=pltpu.CompilerParams(
            collective_id=0, has_side_effects=True, vmem_limit_bytes=48 * 1024 * 1024
        ),
    )(
        station_index,
        shape_az,
        chunks(state_in, rows),
        chunks(base_flow, base_rows),
        chunks(forcing_in, rows),
        jnp.asarray(omegas),
        jnp.asarray(inverse_p.T),
        jnp.asarray(slopes.T),
        jnp.asarray(inverse.transpose(2, 0, 1).reshape(ntime, 2 * freqs)),
        jnp.asarray(forward.reshape(2 * freqs, ntime)),
    )

    return tuple(finish(y, nf, per_dev, variables, own_az, radii, rows, count) for y in outs)


def finish(y, nf, per_dev, variables, own_az, radii, rows, count):
    y = y.reshape(nf, rows, radii)[:, :count].reshape(nf, -1, own_az, radii)
    return y.transpose(1, 0, 2, 3).reshape(2, per_dev, variables, nf * own_az, radii)


MESH = pl.DeviceIdType.MESH


def solution(mesh):
    return jax.shard_map(
        per_device,
        mesh=mesh,
        in_specs=(
            P(None, "freq", None, "plane", None),
            P(None, "freq", None, "plane", None),
            P("freq", None, "plane", None),
            P(),
            P(),
        ),
        out_specs=(P(None, "freq", None, "plane", None), P(None, "freq", None, "plane", None)),
        check_vma=False,
    )
```

```python
import functools
import math

import jax
import jax.numpy as jnp
import numpy as np
from jax import lax
from jax.experimental import pallas as pl
from jax.experimental.pallas import tpu as pltpu
from jax.sharding import PartitionSpec as P

SWEEPS = 4
STEPS = 2


SIDE_WEIGHT = 1.25
MARCH_WEIGHT = 4.0
DIAG_SHIFT = 4.0
ADVECT_SCALE = 0.5
BASE_SCALE = 0.5


def radial_tables(radius_count):
    indices = np.arange(radius_count)
    angles = math.pi * indices / (radius_count - 1)
    nodes = np.cos(angles)
    weights = np.where((indices == 0) | (indices == radius_count - 1), 2.0, 1.0)
    parity = 1.0 - 2.0 * ((indices[:, None] + indices[None, :]) % 2)
    offdiag = indices[:, None] != indices[None, :]
    spacing = np.where(offdiag, nodes[:, None] - nodes[None, :], 1.0)
    entries = np.where(offdiag, weights[:, None] / weights[None, :] * parity / spacing, 0.0)
    entries = entries - np.diag(entries.sum(axis=1))
    slopes = np.sin(angles)[:, None] * entries / (radius_count - 1)
    system = slopes.T @ slopes + DIAG_SHIFT * np.eye(radius_count)
    return slopes.astype(np.float32), np.linalg.inv(system).astype(np.float32)


def transform_tables(mode_ids, freqs, ntime):
    time_ids = np.arange(ntime)
    angles = 2.0 * math.pi * (mode_ids[:, None] * time_ids[None, :] % ntime) / ntime
    stacked = np.stack([np.cos(angles), -np.sin(angles)])
    return (
        (stacked / math.sqrt(freqs)).astype(np.float32),
        (stacked / math.sqrt(ntime)).astype(np.float32),
    )


def chevron(lobe_count, azimuths, start_az, total_az):
    position = start_az + jnp.arange(azimuths)
    phases = lobe_count[0] * position % total_az
    return 1.0 + 0.5 * jnp.cos(2.0 * math.pi * phases.astype(jnp.float32) / total_az)


def halves(x):
    high = x.astype(jnp.bfloat16)
    return high, (x - high.astype(jnp.float32)).astype(jnp.bfloat16)


def right_table(table):
    high, low = np_halves(table)
    return jnp.asarray(np.tile(np.concatenate([high, low], axis=1), (2, 1)))


def left_table(table):
    high, low = np_halves(table)
    return jnp.asarray(np.concatenate([high, high, low, low], axis=1))


def np_halves(table):
    high = table.astype(jnp.bfloat16)
    return high, (table - high.astype(np.float32)).astype(jnp.bfloat16)


def times_right(x, table):
    width = table.shape[1] // 2
    y = jnp.dot(jnp.concatenate(halves(x), axis=1), table, preferred_element_type=jnp.float32)
    return y[:, :width] + y[:, width:]


def times_left(table, x):
    high, low = halves(x)
    return jnp.dot(
        table,
        jnp.concatenate([high, low, high, low], axis=0),
        preferred_element_type=jnp.float32,
    )


def block_of(f, p, nf):
    j = f
    if nf % 4 == 0:
        z, y, x = f // 4, (f // 2) % 2, f % 2
        r = 2 * y + (x + y) % 2
        j = 4 * z + r + (z % 2) * (3 - 2 * r)
    return j + (p % 2) * (nf - 1 - 2 * j)


def freq_of(block, p, nf):
    j = block + (p % 2) * (nf - 1 - 2 * block)
    if nf % 4 == 0:
        z, r = j // 4, j % 4
        r = r + (z % 2) * (3 - 2 * r)
        y = r // 2
        return 4 * z + 2 * y + (r + y) % 2
    return j


def march(
    dims,
    station_ref,
    shape_ref,
    rate_ref,
    state_ref,
    s_base,
    forcing_ref,
    omega_ref,
    qt_ref,
    st_ref,
    inv_ref,
    fwd_ref,
    g_state,
    g_forcing,
    r_state,
    r_base,
    s_state,
    s_w,
    r_w,
    plane_w,
    x_one,
    b_one,
    edge_out,
    edge_in,
    x_ref,
    b_ref,
    f_ref,
    w_ref,
    o_state,
    o_forcing,
    send_sem,
    recv_sem,
    own_sem,
    halo_send,
    halo_recv,
    edge_send,
    edge_recv,
    load_sem,
):
    nf, planes, own_az, variables, per_dev, radii, stored, rows, base_rows, w_rows = dims
    freqs = nf * per_dev
    span = nf * own_az
    runs = 2 * per_dev * variables
    ntime = inv_ref.shape[0]
    half = variables * freqs
    me = lax.axis_index("freq")
    plane = lax.axis_index("plane")
    block = block_of(me, plane, nf)
    ring = nf * planes
    here = plane * nf + block
    right, left = (here + 1) % ring, (here + ring - 1) % ring

    def at_ring(g):
        p = g // nf
        return {"freq": freq_of(g % nf, p, nf), "plane": p}

    right_id, left_id = at_ring(right), at_ring(left)

    barrier = pltpu.get_barrier_semaphore()

    @pl.loop(1, nf)
    def _(d):
        pl.semaphore_signal(
            barrier, inc=1, device_id={"freq": (me + d) % nf, "plane": plane}, device_id_type=MESH
        )

    beyond = {"freq": me, "plane": (plane + 1) % planes}
    behind = {"freq": me, "plane": (plane + planes - 1) % planes}
    for target in (right_id, left_id, beyond, behind):
        pl.semaphore_signal(barrier, inc=1, device_id=target, device_id_type=MESH)
    load_state = pltpu.make_async_copy(state_ref, x_one.at[0, :, pl.ds(8, span), :], load_sem.at[0])
    load_forcing = pltpu.make_async_copy(forcing_ref, b_one, load_sem.at[1])
    load_state.start()
    load_forcing.start()
    pl.semaphore_wait(barrier, nf + 3)

    def exchange(k, source, landing, index_to, mine, size, first):
        def copy(d):
            other = (me + d) % nf
            src = source.at[pl.ds(pl.multiple_of(index_to(other) * size, 8), size), :]
            dst = landing.at[pl.ds(pl.multiple_of(mine * size, 8), size), :]
            return pltpu.make_async_remote_copy(
                src_ref=src,
                dst_ref=dst,
                send_sem=send_sem.at[k, d],
                recv_sem=recv_sem.at[k, d],
                device_id={"freq": other, "plane": plane},
                device_id_type=MESH,
            )

        own = pltpu.make_async_copy(
            source.at[pl.ds(pl.multiple_of(index_to(me) * size, 8), size), :],
            landing.at[pl.ds(pl.multiple_of(mine * size, 8), size), :],
            own_sem.at[k],
        )
        if first:

            @pl.loop(1, nf)
            def _(d):
                copy(d).start()

            own.start()
        else:

            @pl.loop(1, nf)
            def _(d):
                copy(d).wait()

            own.wait()

    def to_block(f):
        return block_of(f, plane, nf)

    def to_freq(f):
        return f

    base_args = (1, s_base, r_base, to_block, me, base_rows)
    state_args = (0, s_state, r_state, to_block, me, rows)
    w_args = (2, s_w, r_w, lambda f: 0, block, w_rows)
    out_state_args = (3, o_state, g_state, to_freq, block, rows)
    out_forcing_args = (4, o_forcing, g_forcing, to_freq, block, rows)
    exchange(*base_args, True)

    def halo_copies(e):
        slot = e % 2
        return (
            pltpu.make_async_remote_copy(
                src_ref=x_ref.at[slot, own_az],
                dst_ref=x_ref.at[slot, 0],
                send_sem=halo_send.at[0, e],
                recv_sem=halo_recv.at[0, e],
                device_id=right_id,
                device_id_type=MESH,
            ),
            pltpu.make_async_remote_copy(
                src_ref=x_ref.at[slot, 1],
                dst_ref=x_ref.at[slot, own_az + 1],
                send_sem=halo_send.at[1, e],
                recv_sem=halo_recv.at[1, e],
                device_id=left_id,
                device_id_type=MESH,
            ),
        )

    def place(a, c, v, kk):
        return ((c * variables + v) * per_dev + kk) * nf

    def packed_row(a, c, v, kk):
        return ((c * per_dev + kk) * variables + v) * own_az + a

    def each_run(visit):
        @pl.loop(0, own_az)
        def _(a):
            for c in range(2):
                for v in range(variables):
                    for kk in range(per_dev):
                        visit(a, place(a, c, v, kk), packed_row(a, c, v, kk))

    def in_row(a, c, v, kk):
        return ((c * per_dev + kk) * variables + v) * own_az + a

    def edge_copies(e):
        return [
            pltpu.make_async_remote_copy(
                src_ref=edge_out.at[e, side],
                dst_ref=edge_in.at[e, side],
                send_sem=edge_send.at[side, e],
                recv_sem=edge_recv.at[side, e],
                device_id=target,
                device_id_type=MESH,
            )
            for side, target in ((0, beyond), (1, behind))
        ]

    def send_edges(slot, e):
        for m in range(runs):
            edge_out[e, 0, pl.ds(m, 1), :] = x_one[slot, m, pl.ds(7 + span, 1), :]
            edge_out[e, 1, pl.ds(m, 1), :] = x_one[slot, m, pl.ds(8, 1), :]
        for copy in edge_copies(e):
            copy.start()

    load_state.wait()
    send_edges(0, 0)
    load_forcing.wait()

    @pl.loop(0, runs)
    def _(m):
        b_one[m] = MARCH_WEIGHT * x_one[0, m, pl.ds(8, span), :] + b_one[m]

    exchange(*base_args, False)
    for station in range(STEPS):
        wanted = station_ref[station]

        @pl.loop(0, own_az)
        def _(a):
            for v in range(variables):
                scaled = (BASE_SCALE * shape_ref[a]) * r_base[
                    pl.ds(
                        (wanted // stored) * base_rows
                        + ((wanted % stored) * variables + v) * own_az
                        + a,
                        1,
                    ),
                    :,
                ]
                if station == 0:
                    s_w[pl.ds(v * own_az + a, 1), :] = scaled
                else:
                    w_ref[(station - 1) * own_az + a, pl.ds(v, 1), :] = scaled

        if station == 0:
            exchange(*w_args, True)
    exchange(*w_args, False)

    @pl.loop(0, nf)
    def _(j):
        for v in range(variables):
            plane_w[v, pl.ds(j * own_az, own_az), :] = r_w[pl.ds(j * w_rows + v * own_az, own_az), :]

    @pl.loop(0, SWEEPS)
    def _(e):
        src, dst = e % 2, (e + 1) % 2
        for copy in edge_copies(e):
            copy.wait()
        for m in range(runs):
            x_one[src, m, pl.ds(7, 1), :] = edge_in[e, 0, pl.ds(m, 1), :]
            x_one[src, m, pl.ds(8 + span, 1), :] = edge_in[e, 1, pl.ds(m, 1), :]
        for kk in range(per_dev):
            rate = rate_ref[kk]

            @pl.loop(0, variables)
            def _(v):
                w = plane_w[v]
                at = [(c * per_dev + kk) * variables + v for c in range(2)]
                real, imag = [x_one[src, m, pl.ds(8, span), :] for m in at]
                mixing = (w * real - rate * imag, w * imag + rate * real)
                summed = [
                    SIDE_WEIGHT
                    * (x_one[src, m, pl.ds(7, span), :] + x_one[src, m, pl.ds(9, span), :])
                    + b_one[m]
                    - mixed
                    for m, mixed in zip(at, mixing)
                ]
                q = times_right(jnp.concatenate(summed, axis=0), qt_ref[...])
                x_one[dst, at[0], pl.ds(8, span), :] = q[:span]
                x_one[dst, at[1], pl.ds(8, span), :] = q[span:]

        @pl.when(e < SWEEPS - 1)
        def _():
            send_edges(dst, e + 1)

    settled = SWEEPS % 2

    @pl.loop(0, nf)
    def _(j):
        for m in range(runs):
            s_state[pl.ds(j * rows + m * own_az, own_az), :] = x_one[
                settled, m, pl.ds(8 + j * own_az, own_az), :
            ]

    exchange(*state_args, True)
    exchange(*state_args, False)

    def unpack_state(a, start, row):
        x_ref[0, a + 1, pl.ds(start, nf), :] = r_state[pl.ds(row, nf, stride=rows), :]

    each_run(unpack_state)
    for copy in halo_copies(0):
        copy.start()
    omega = omega_ref[...][None]
    flat = (2 * half, radii)
    cube = (variables, freqs, radii)

    def sweep_slab(src, dst, a, station):
        x = x_ref[src, a + 1]
        beside = SIDE_WEIGHT * (x_ref[src, a] + x_ref[src, a + 2]) + b_ref[a]
        real, imag = x[:half].reshape(cube), x[half:].reshape(cube)
        w = w_ref[(station - 1) * own_az + a][:variables][:, None, :]
        mixing = jnp.concatenate([w * real - omega * imag, w * imag + omega * real], axis=0)
        summed = beside - mixing.reshape(flat)
        x_ref[dst, a + 1] = times_right(summed, qt_ref[...])

    def advect_slab(slot, a, final):
        x = x_ref[slot, a + 1]
        beside = 0.5 * (x_ref[slot, a + 2] - x_ref[slot, a])

        def lanes(y):
            return [
                jnp.concatenate(
                    [
                        y[v * freqs : (v + 1) * freqs],
                        y[half + v * freqs : half + (v + 1) * freqs],
                    ],
                    axis=0,
                )
                for v in range(variables)
            ]

        both = jnp.concatenate(lanes(x) + lanes(beside), axis=1)
        in_time = times_left(inv_ref[...], both)
        u = [in_time[:, v * radii : (v + 1) * radii] for v in range(variables)]
        ua = [
            in_time[:, (variables + v) * radii : (variables + v + 1) * radii]
            for v in range(variables)
        ]
        radial = times_right(jnp.concatenate(u, axis=0), st_ref[...])
        ur = [radial[v * ntime : (v + 1) * ntime] for v in range(variables)]
        n = [u[1] * ur[v] + u[2] * ua[v] for v in range(variables)]
        n[0] = n[0] + u[0] * (ur[1] + ua[2])
        source = -ADVECT_SCALE * jnp.concatenate(n, axis=1)
        spectral = times_left(fwd_ref[...], source)
        forcing = jnp.concatenate(
            [
                spectral[c * freqs : (c + 1) * freqs, v * radii : (v + 1) * radii]
                for c in range(2)
                for v in range(variables)
            ],
            axis=0,
        )
        if final:
            f_ref[a] = forcing
        else:
            b_ref[a] = MARCH_WEIGHT * x + forcing

    def advect_all(slot, e, final):
        @pl.loop(1, own_az - 1)
        def _(a):
            advect_slab(slot, a, final)

        for copy in halo_copies(e):
            copy.wait()
        advect_slab(slot, 0, final)
        if own_az > 1:
            advect_slab(slot, own_az - 1, final)

    advect_all(0, 0, False)
    for station in range(1, STEPS):

        @pl.loop(0, SWEEPS)
        def _(sweep):
            e = (station - 1) * SWEEPS + sweep
            src, dst = e % 2, (e + 1) % 2

            @pl.when(sweep > 0)
            def _():
                for copy in halo_copies(e):
                    copy.wait()

            sweep_slab(src, dst, 0, station)
            if own_az > 1:
                sweep_slab(src, dst, own_az - 1, station)
            for copy in halo_copies(e + 1):
                copy.start()

            @pl.loop(1, own_az - 1)
            def _(a):
                sweep_slab(src, dst, a, station)

        last = station * SWEEPS
        slot = last % 2
        final = station == STEPS - 1
        if final:

            def pack_state(a, start, row):
                o_state[pl.ds(row, nf, stride=rows), :] = x_ref[slot, a + 1, pl.ds(start, nf), :]

            each_run(pack_state)
            exchange(*out_state_args, True)

        advect_all(slot, last, final)

    def pack_forcing(a, start, row):
        o_forcing[pl.ds(row, nf, stride=rows), :] = f_ref[a, pl.ds(start, nf), :]

    each_run(pack_forcing)
    exchange(*out_forcing_args, True)
    exchange(*out_state_args, False)
    exchange(*out_forcing_args, False)


def per_device(state_in, forcing_in, base_flow, station_index, lobe_count):
    _, per_dev, variables, span_az, radii = state_in.shape
    nf = lax.axis_size("freq")
    planes = lax.axis_size("plane")
    freqs = per_dev * nf
    ntime = 3 * freqs // 2
    own_az = span_az // nf
    stored = base_flow.shape[0]
    slopes, inverse_p = radial_tables(radii)
    mode_ids = (np.arange(nf)[None, :] * per_dev + np.arange(per_dev)[:, None]).reshape(-1)
    inverse, forward = transform_tables(mode_ids, freqs, ntime)
    omegas = np.broadcast_to((0.5 * mode_ids / freqs).astype(np.float32)[:, None], (freqs, radii))
    plane = lax.axis_index("plane")
    block = block_of(lax.axis_index("freq"), plane, nf)
    shape_az = chevron(lobe_count, own_az, plane * span_az + block * own_az, span_az * planes)

    def padded_rows(count):
        return -(-count // 8) * 8

    def chunks(x, size):
        x = x.reshape(-1, nf, own_az, radii).transpose(1, 0, 2, 3).reshape(nf, -1, radii)
        x = jnp.pad(x, ((0, 0), (0, size - x.shape[1]), (0, 0)))
        return x.reshape(nf * size, radii)

    count = 2 * per_dev * variables * own_az
    rows = padded_rows(count)
    base_rows = padded_rows(stored * variables * own_az)
    w_rows = padded_rows(variables * own_az)
    dims = (nf, planes, own_az, variables, per_dev, radii, stored, rows, base_rows, w_rows)
    half = variables * freqs
    exchanges = (STEPS - 1) * SWEEPS + 1
    runs = 2 * per_dev * variables
    edge_rows = padded_rows(runs)
    first_mode = lax.axis_index("freq") * per_dev
    rates = 0.5 * (first_mode + jnp.arange(per_dev)).astype(jnp.float32) / freqs
    vmem = pl.BlockSpec(memory_space=pltpu.VMEM)
    smem = pl.BlockSpec(memory_space=pltpu.SMEM)
    anywhere = pl.BlockSpec(memory_space=pl.ANY)
    packed = (nf * rows, radii)
    f32 = jnp.float32
    outs = pl.pallas_call(
        functools.partial(march, dims),
        out_shape=[jax.ShapeDtypeStruct(packed, f32)] * 2,
        in_specs=[smem, smem, smem, anywhere, anywhere, anywhere] + [vmem] * 5,
        out_specs=[anywhere, anywhere],
        scratch_shapes=[
            pltpu.VMEM(packed, f32),
            pltpu.VMEM((nf * base_rows, radii), f32),
            pltpu.VMEM(packed, f32),
            pltpu.VMEM((w_rows, radii), f32),
            pltpu.VMEM((nf * w_rows, radii), f32),
            pltpu.VMEM((variables, span_az, radii), f32),
            pltpu.VMEM((2, runs, span_az + 16, radii), f32),
            pltpu.VMEM((runs, span_az, radii), f32),
            pltpu.VMEM((SWEEPS, 2, edge_rows, radii), f32),
            pltpu.VMEM((SWEEPS, 2, edge_rows, radii), f32),
            pltpu.VMEM((2, own_az + 2, 2 * half, radii), f32),
            pltpu.VMEM((own_az, 2 * half, radii), f32),
            pltpu.VMEM((own_az, 2 * half, radii), f32),
            pltpu.VMEM(((STEPS - 1) * own_az, padded_rows(variables), radii), f32),
            pltpu.VMEM(packed, f32),
            pltpu.VMEM(packed, f32),
            pltpu.SemaphoreType.DMA((5, nf)),
            pltpu.SemaphoreType.DMA((5, nf)),
            pltpu.SemaphoreType.DMA((5,)),
            pltpu.SemaphoreType.DMA((2, exchanges)),
            pltpu.SemaphoreType.DMA((2, exchanges)),
            pltpu.SemaphoreType.DMA((2, SWEEPS)),
            pltpu.SemaphoreType.DMA((2, SWEEPS)),
            pltpu.SemaphoreType.DMA((2,)),
        ],
        compiler_params=pltpu.CompilerParams(
            collective_id=0, has_side_effects=True, vmem_limit_bytes=48 * 1024 * 1024
        ),
    )(
        station_index,
        shape_az,
        rates,
        state_in.reshape(runs, span_az, radii),
        chunks(base_flow, base_rows),
        forcing_in.reshape(runs, span_az, radii),
        jnp.asarray(omegas),
        right_table(inverse_p.T),
        right_table(slopes.T),
        left_table(inverse.transpose(2, 0, 1).reshape(ntime, 2 * freqs)),
        left_table(forward.reshape(2 * freqs, ntime)),
    )

    return tuple(finish(y, nf, per_dev, variables, own_az, radii, rows, count) for y in outs)


def finish(y, nf, per_dev, variables, own_az, radii, rows, count):
    y = y.reshape(nf, rows, radii)[:, :count].reshape(nf, -1, own_az, radii)
    return y.transpose(1, 0, 2, 3).reshape(2, per_dev, variables, nf * own_az, radii)


MESH = pl.DeviceIdType.MESH


def solution(mesh):
    return jax.shard_map(
        per_device,
        mesh=mesh,
        in_specs=(
            P(None, "freq", None, "plane", None),
            P(None, "freq", None, "plane", None),
            P("freq", None, "plane", None),
            P(),
            P(),
        ),
        out_specs=(P(None, "freq", None, "plane", None), P(None, "freq", None, "plane", None)),
        check_vma=False,
    )
```

```python
import functools
import math

import jax
import jax.numpy as jnp
import numpy as np
from jax import lax
from jax.experimental import pallas as pl
from jax.experimental.pallas import tpu as pltpu
from jax.sharding import PartitionSpec as P

SWEEPS = 4
STEPS = 2


SIDE_WEIGHT = 1.25
MARCH_WEIGHT = 4.0
DIAG_SHIFT = 4.0
ADVECT_SCALE = 0.5
BASE_SCALE = 0.5


def radial_tables(radius_count):
    indices = np.arange(radius_count)
    angles = math.pi * indices / (radius_count - 1)
    nodes = np.cos(angles)
    weights = np.where((indices == 0) | (indices == radius_count - 1), 2.0, 1.0)
    parity = 1.0 - 2.0 * ((indices[:, None] + indices[None, :]) % 2)
    offdiag = indices[:, None] != indices[None, :]
    spacing = np.where(offdiag, nodes[:, None] - nodes[None, :], 1.0)
    entries = np.where(offdiag, weights[:, None] / weights[None, :] * parity / spacing, 0.0)
    entries = entries - np.diag(entries.sum(axis=1))
    slopes = np.sin(angles)[:, None] * entries / (radius_count - 1)
    system = slopes.T @ slopes + DIAG_SHIFT * np.eye(radius_count)
    return slopes.astype(np.float32), np.linalg.inv(system).astype(np.float32)


def transform_tables(mode_ids, freqs, ntime):
    time_ids = np.arange(ntime)
    angles = 2.0 * math.pi * (mode_ids[:, None] * time_ids[None, :] % ntime) / ntime
    stacked = np.stack([np.cos(angles), -np.sin(angles)])
    return (
        (stacked / math.sqrt(freqs)).astype(np.float32),
        (stacked / math.sqrt(ntime)).astype(np.float32),
    )


def chevron(lobe_count, azimuths, start_az, total_az):
    position = start_az + jnp.arange(azimuths)
    phases = lobe_count[0] * position % total_az
    return 1.0 + 0.5 * jnp.cos(2.0 * math.pi * phases.astype(jnp.float32) / total_az)


def halves(x):
    high = x.astype(jnp.bfloat16)
    return high, (x - high.astype(jnp.float32)).astype(jnp.bfloat16)


def right_table(table):
    high, low = np_halves(table)
    return jnp.asarray(np.tile(np.concatenate([high, low], axis=1), (2, 1)))


def left_table(table):
    high, low = np_halves(table)
    return jnp.asarray(np.concatenate([high, high, low, low], axis=1))


def np_halves(table):
    high = table.astype(jnp.bfloat16)
    return high, (table - high.astype(np.float32)).astype(jnp.bfloat16)


def times_right(x, table):
    width = table.shape[1] // 2
    y = jnp.dot(jnp.concatenate(halves(x), axis=1), table, preferred_element_type=jnp.float32)
    return y[:, :width] + y[:, width:]


def times_left(table, x):
    high, low = halves(x)
    return jnp.dot(
        table,
        jnp.concatenate([high, low, high, low], axis=0),
        preferred_element_type=jnp.float32,
    )


def ring_of(f, p, nf, planes):
    at = f
    if nf % 4 == 0:
        high = nf // 4
        z, y, x = f // 4, (f // 2) % 2, f % 2
        column = 2 * y + (x + y) % 2
        at = column * high + z + (column % 2) * (high - 1 - 2 * z)
    return at * planes + p


def device_of(g, nf, planes):
    at = g // planes
    f = at
    if nf % 4 == 0:
        high = nf // 4
        column, z = at // high, at % high
        z = z + (column % 2) * (high - 1 - 2 * z)
        y = column // 2
        f = 4 * z + 2 * y + (column + y) % 2
    return f, g % planes


def march(
    dims,
    station_ref,
    shape_ref,
    rate_ref,
    state_ref,
    s_base,
    forcing_ref,
    far_omega,
    far_qt,
    far_st,
    far_inv,
    far_fwd,
    g_state,
    g_forcing,
    r_state,
    r_base,
    s_state,
    s_w,
    r_w,
    plane_w,
    x_one,
    b_one,
    edge_out,
    edge_in,
    x_ref,
    b_ref,
    f_ref,
    w_ref,
    o_state,
    o_forcing,
    send_sem,
    recv_sem,
    own_sem,
    halo_send,
    halo_recv,
    edge_send,
    edge_recv,
    load_sem,
    omega_ref,
    qt_ref,
    st_ref,
    inv_ref,
    fwd_ref,
    table_sem,
):
    nf, planes, own_az, variables, per_dev, radii, stored, rows, base_rows, w_rows = dims
    freqs = nf * per_dev
    span = nf * own_az
    runs = 2 * per_dev * variables
    ntime = inv_ref.shape[0]
    half = variables * freqs
    me = lax.axis_index("freq")
    plane = lax.axis_index("plane")
    ring = nf * planes
    here = ring_of(me, plane, nf, planes)
    part, block = here // nf, here % nf

    def named(device):
        return {"freq": device[0], "plane": device[1]}

    right_id = named(device_of((here + 1) % ring, nf, planes))
    left_id = named(device_of((here + ring - 1) % ring, nf, planes))
    barrier = pltpu.get_barrier_semaphore()

    @pl.loop(1, ring)
    def _(d):
        other = (me * planes + plane + d) % ring
        pl.semaphore_signal(
            barrier,
            inc=1,
            device_id={"freq": other // planes, "plane": other % planes},
            device_id_type=MESH,
        )

    beyond = {"freq": me, "plane": (plane + 1) % planes}
    behind = {"freq": me, "plane": (plane + planes - 1) % planes}
    load_state = pltpu.make_async_copy(state_ref, x_one.at[0, :, pl.ds(8, span), :], load_sem.at[0])
    load_forcing = pltpu.make_async_copy(forcing_ref, b_one, load_sem.at[1])
    load_state.start()
    load_forcing.start()
    tables = [
        pltpu.make_async_copy(far, near, table_sem.at[i])
        for i, (far, near) in enumerate(
            (
                (far_omega, omega_ref),
                (far_qt, qt_ref),
                (far_st, st_ref),
                (far_inv, inv_ref),
                (far_fwd, fwd_ref),
            )
        )
    ]
    for table in tables:
        table.start()
    pl.semaphore_wait(barrier, ring - 1)

    def owner(i):
        return device_of(plane * nf + i, nf, planes)

    def holder(i):
        return i, part

    def is_me(device):
        return (device[0] == me) & (device[1] == plane)

    def exchange(k, source, landing, target, origin, pick, mine, size, first):
        def rows_of(ref, i):
            return ref.at[pl.ds(pl.multiple_of(i * size, 8), size), :]

        def copy(i):
            return pltpu.make_async_remote_copy(
                src_ref=rows_of(source, pick(i)),
                dst_ref=rows_of(landing, mine),
                send_sem=send_sem.at[k, i],
                recv_sem=recv_sem.at[k, mine],
                device_id=named(target(i)),
                device_id_type=MESH,
            )

        def arrival(i):
            return pltpu.make_async_remote_copy(
                src_ref=rows_of(landing, i),
                dst_ref=rows_of(landing, i),
                send_sem=send_sem.at[k, i],
                recv_sem=recv_sem.at[k, i],
                device_id=named(origin(i)),
                device_id_type=MESH,
            )

        def own(i):
            return pltpu.make_async_copy(
                rows_of(source, pick(i)), rows_of(landing, mine), own_sem.at[k]
            )

        @pl.loop(0, nf)
        def _(d):
            i = (d + me) % nf
            stays = is_me(target(i))

            @pl.when(stays)
            def _():
                if first:
                    own(i).start()
                else:
                    own(i).wait()

            @pl.when(jnp.logical_not(stays))
            def _():
                if first:
                    copy(i).start()
                else:
                    copy(i).wait_send()

            if not first:

                @pl.when(jnp.logical_not(is_me(origin(i))))
                def _():
                    arrival(i).wait_recv()

    def same(i):
        return i

    base_args = (1, s_base, r_base, owner, holder, same, me, base_rows)
    state_args = (0, s_state, r_state, owner, holder, same, me, rows)
    w_args = (2, s_w, r_w, holder, owner, lambda i: 0, block, w_rows)
    out_state_args = (3, o_state, g_state, holder, owner, same, block, rows)
    out_forcing_args = (4, o_forcing, g_forcing, holder, owner, same, block, rows)
    exchange(*base_args, True)

    def halo_copies(e):
        slot = e % 2
        return (
            pltpu.make_async_remote_copy(
                src_ref=x_ref.at[slot, own_az],
                dst_ref=x_ref.at[slot, 0],
                send_sem=halo_send.at[0, e],
                recv_sem=halo_recv.at[0, e],
                device_id=right_id,
                device_id_type=MESH,
            ),
            pltpu.make_async_remote_copy(
                src_ref=x_ref.at[slot, 1],
                dst_ref=x_ref.at[slot, own_az + 1],
                send_sem=halo_send.at[1, e],
                recv_sem=halo_recv.at[1, e],
                device_id=left_id,
                device_id_type=MESH,
            ),
        )

    def place(a, c, v, kk):
        return ((c * variables + v) * per_dev + kk) * nf

    def packed_row(a, c, v, kk):
        return ((c * per_dev + kk) * variables + v) * own_az + a

    def each_run(visit):
        @pl.loop(0, own_az)
        def _(a):
            for c in range(2):
                for v in range(variables):
                    for kk in range(per_dev):
                        visit(a, place(a, c, v, kk), packed_row(a, c, v, kk))

    def in_row(a, c, v, kk):
        return ((c * per_dev + kk) * variables + v) * own_az + a

    def edge_copies(e):
        return [
            pltpu.make_async_remote_copy(
                src_ref=edge_out.at[e, side],
                dst_ref=edge_in.at[e, side],
                send_sem=edge_send.at[side, e],
                recv_sem=edge_recv.at[side, e],
                device_id=target,
                device_id_type=MESH,
            )
            for side, target in ((0, beyond), (1, behind))
        ]

    def send_edges(slot, e):
        for m in range(runs):
            edge_out[e, 0, pl.ds(m, 1), :] = x_one[slot, m, pl.ds(7 + span, 1), :]
            edge_out[e, 1, pl.ds(m, 1), :] = x_one[slot, m, pl.ds(8, 1), :]
        for copy in edge_copies(e):
            copy.start()

    for table in tables:
        table.wait()
    load_state.wait()
    send_edges(0, 0)
    load_forcing.wait()

    @pl.loop(0, runs)
    def _(m):
        b_one[m] = MARCH_WEIGHT * x_one[0, m, pl.ds(8, span), :] + b_one[m]

    exchange(*base_args, False)
    for station in range(STEPS):
        wanted = station_ref[station]

        @pl.loop(0, own_az)
        def _(a):
            for v in range(variables):
                scaled = (BASE_SCALE * shape_ref[a]) * r_base[
                    pl.ds(
                        (wanted // stored) * base_rows
                        + ((wanted % stored) * variables + v) * own_az
                        + a,
                        1,
                    ),
                    :,
                ]
                if station == 0:
                    s_w[pl.ds(v * own_az + a, 1), :] = scaled
                else:
                    w_ref[(station - 1) * own_az + a, pl.ds(v, 1), :] = scaled

        if station == 0:
            exchange(*w_args, True)
    exchange(*w_args, False)

    @pl.loop(0, nf)
    def _(j):
        for v in range(variables):
            plane_w[v, pl.ds(j * own_az, own_az), :] = r_w[pl.ds(j * w_rows + v * own_az, own_az), :]

    @pl.loop(0, SWEEPS)
    def _(e):
        src, dst = e % 2, (e + 1) % 2
        for copy in edge_copies(e):
            copy.wait()
        for m in range(runs):
            x_one[src, m, pl.ds(7, 1), :] = edge_in[e, 0, pl.ds(m, 1), :]
            x_one[src, m, pl.ds(8 + span, 1), :] = edge_in[e, 1, pl.ds(m, 1), :]
        for kk in range(per_dev):
            rate = rate_ref[kk]

            @pl.loop(0, variables)
            def _(v):
                w = plane_w[v]
                at = [(c * per_dev + kk) * variables + v for c in range(2)]
                real, imag = [x_one[src, m, pl.ds(8, span), :] for m in at]
                mixing = (w * real - rate * imag, w * imag + rate * real)
                summed = [
                    SIDE_WEIGHT
                    * (x_one[src, m, pl.ds(7, span), :] + x_one[src, m, pl.ds(9, span), :])
                    + b_one[m]
                    - mixed
                    for m, mixed in zip(at, mixing)
                ]
                q = times_right(jnp.concatenate(summed, axis=0), qt_ref[...])
                x_one[dst, at[0], pl.ds(8, span), :] = q[:span]
                x_one[dst, at[1], pl.ds(8, span), :] = q[span:]

        @pl.when(e < SWEEPS - 1)
        def _():
            send_edges(dst, e + 1)

    settled = SWEEPS % 2

    @pl.loop(0, nf)
    def _(j):
        for m in range(runs):
            s_state[pl.ds(j * rows + m * own_az, own_az), :] = x_one[
                settled, m, pl.ds(8 + j * own_az, own_az), :
            ]

    exchange(*state_args, True)
    exchange(*state_args, False)

    def unpack_state(a, start, row):
        x_ref[0, a + 1, pl.ds(start, nf), :] = r_state[pl.ds(row, nf, stride=rows), :]

    each_run(unpack_state)
    for copy in halo_copies(0):
        copy.start()
    omega = omega_ref[...][None]
    flat = (2 * half, radii)
    cube = (variables, freqs, radii)

    def sweep_slab(src, dst, a, station):
        x = x_ref[src, a + 1]
        beside = SIDE_WEIGHT * (x_ref[src, a] + x_ref[src, a + 2]) + b_ref[a]
        real, imag = x[:half].reshape(cube), x[half:].reshape(cube)
        w = w_ref[(station - 1) * own_az + a][:variables][:, None, :]
        mixing = jnp.concatenate([w * real - omega * imag, w * imag + omega * real], axis=0)
        summed = beside - mixing.reshape(flat)
        x_ref[dst, a + 1] = times_right(summed, qt_ref[...])

    def advect_slab(slot, a, final):
        x = x_ref[slot, a + 1]
        beside = 0.5 * (x_ref[slot, a + 2] - x_ref[slot, a])

        def lanes(y):
            return [
                jnp.concatenate(
                    [
                        y[v * freqs : (v + 1) * freqs],
                        y[half + v * freqs : half + (v + 1) * freqs],
                    ],
                    axis=0,
                )
                for v in range(variables)
            ]

        both = jnp.concatenate(lanes(x) + lanes(beside), axis=1)
        in_time = times_left(inv_ref[...], both)
        u = [in_time[:, v * radii : (v + 1) * radii] for v in range(variables)]
        ua = [
            in_time[:, (variables + v) * radii : (variables + v + 1) * radii]
            for v in range(variables)
        ]
        radial = times_right(jnp.concatenate(u, axis=0), st_ref[...])
        ur = [radial[v * ntime : (v + 1) * ntime] for v in range(variables)]
        n = [u[1] * ur[v] + u[2] * ua[v] for v in range(variables)]
        n[0] = n[0] + u[0] * (ur[1] + ua[2])
        source = -ADVECT_SCALE * jnp.concatenate(n, axis=1)
        spectral = times_left(fwd_ref[...], source)
        forcing = jnp.concatenate(
            [
                spectral[c * freqs : (c + 1) * freqs, v * radii : (v + 1) * radii]
                for c in range(2)
                for v in range(variables)
            ],
            axis=0,
        )
        if final:
            f_ref[a] = forcing
        else:
            b_ref[a] = MARCH_WEIGHT * x + forcing

    def advect_all(slot, e, final):
        @pl.loop(1, own_az - 1)
        def _(a):
            advect_slab(slot, a, final)

        for copy in halo_copies(e):
            copy.wait()
        advect_slab(slot, 0, final)
        if own_az > 1:
            advect_slab(slot, own_az - 1, final)

    advect_all(0, 0, False)
    for station in range(1, STEPS):

        @pl.loop(0, SWEEPS)
        def _(sweep):
            e = (station - 1) * SWEEPS + sweep
            src, dst = e % 2, (e + 1) % 2

            @pl.when(sweep > 0)
            def _():
                for copy in halo_copies(e):
                    copy.wait()

            sweep_slab(src, dst, 0, station)
            if own_az > 1:
                sweep_slab(src, dst, own_az - 1, station)
            for copy in halo_copies(e + 1):
                copy.start()

            @pl.loop(1, own_az - 1)
            def _(a):
                sweep_slab(src, dst, a, station)

        last = station * SWEEPS
        slot = last % 2
        final = station == STEPS - 1
        if final:

            def pack_state(a, start, row):
                o_state[pl.ds(row, nf, stride=rows), :] = x_ref[slot, a + 1, pl.ds(start, nf), :]

            each_run(pack_state)
            exchange(*out_state_args, True)

        advect_all(slot, last, final)

    def pack_forcing(a, start, row):
        o_forcing[pl.ds(row, nf, stride=rows), :] = f_ref[a, pl.ds(start, nf), :]

    each_run(pack_forcing)
    exchange(*out_forcing_args, True)
    exchange(*out_state_args, False)
    exchange(*out_forcing_args, False)


def per_device(state_in, forcing_in, base_flow, station_index, lobe_count):
    _, per_dev, variables, span_az, radii = state_in.shape
    nf = lax.axis_size("freq")
    planes = lax.axis_size("plane")
    freqs = per_dev * nf
    ntime = 3 * freqs // 2
    own_az = span_az // nf
    stored = base_flow.shape[0]
    slopes, inverse_p = radial_tables(radii)
    mode_ids = (np.arange(nf)[None, :] * per_dev + np.arange(per_dev)[:, None]).reshape(-1)
    inverse, forward = transform_tables(mode_ids, freqs, ntime)
    omegas = np.broadcast_to((0.5 * mode_ids / freqs).astype(np.float32)[:, None], (freqs, radii))
    plane = lax.axis_index("plane")
    here = ring_of(lax.axis_index("freq"), plane, nf, planes)
    shape_az = chevron(lobe_count, own_az, here * own_az, span_az * planes)

    def padded_rows(count):
        return -(-count // 8) * 8

    def chunks(x, size):
        x = x.reshape(-1, nf, own_az, radii).transpose(1, 0, 2, 3).reshape(nf, -1, radii)
        x = jnp.pad(x, ((0, 0), (0, size - x.shape[1]), (0, 0)))
        return x.reshape(nf * size, radii)

    count = 2 * per_dev * variables * own_az
    rows = padded_rows(count)
    base_rows = padded_rows(stored * variables * own_az)
    w_rows = padded_rows(variables * own_az)
    dims = (nf, planes, own_az, variables, per_dev, radii, stored, rows, base_rows, w_rows)
    half = variables * freqs
    exchanges = (STEPS - 1) * SWEEPS + 1
    runs = 2 * per_dev * variables
    edge_rows = padded_rows(runs)
    first_mode = lax.axis_index("freq") * per_dev
    rates = 0.5 * (first_mode + jnp.arange(per_dev)).astype(jnp.float32) / freqs
    smem = pl.BlockSpec(memory_space=pltpu.SMEM)
    anywhere = pl.BlockSpec(memory_space=pl.ANY)
    packed = (nf * rows, radii)
    f32 = jnp.float32
    outs = pl.pallas_call(
        functools.partial(march, dims),
        out_shape=[jax.ShapeDtypeStruct(packed, f32)] * 2,
        in_specs=[smem, smem, smem, anywhere, anywhere, anywhere] + [anywhere] * 5,
        out_specs=[anywhere, anywhere],
        scratch_shapes=[
            pltpu.VMEM(packed, f32),
            pltpu.VMEM((nf * base_rows, radii), f32),
            pltpu.VMEM(packed, f32),
            pltpu.VMEM((w_rows, radii), f32),
            pltpu.VMEM((nf * w_rows, radii), f32),
            pltpu.VMEM((variables, span_az, radii), f32),
            pltpu.VMEM((2, runs, span_az + 16, radii), f32),
            pltpu.VMEM((runs, span_az, radii), f32),
            pltpu.VMEM((SWEEPS, 2, edge_rows, radii), f32),
            pltpu.VMEM((SWEEPS, 2, edge_rows, radii), f32),
            pltpu.VMEM((2, own_az + 2, 2 * half, radii), f32),
            pltpu.VMEM((own_az, 2 * half, radii), f32),
            pltpu.VMEM((own_az, 2 * half, radii), f32),
            pltpu.VMEM(((STEPS - 1) * own_az, padded_rows(variables), radii), f32),
            pltpu.VMEM(packed, f32),
            pltpu.VMEM(packed, f32),
            pltpu.SemaphoreType.DMA((5, nf)),
            pltpu.SemaphoreType.DMA((5, nf)),
            pltpu.SemaphoreType.DMA((5,)),
            pltpu.SemaphoreType.DMA((2, exchanges)),
            pltpu.SemaphoreType.DMA((2, exchanges)),
            pltpu.SemaphoreType.DMA((2, SWEEPS)),
            pltpu.SemaphoreType.DMA((2, SWEEPS)),
            pltpu.SemaphoreType.DMA((2,)),
            pltpu.VMEM((freqs, radii), f32),
            pltpu.VMEM((2 * radii, 2 * radii), jnp.bfloat16),
            pltpu.VMEM((2 * radii, 2 * radii), jnp.bfloat16),
            pltpu.VMEM((ntime, 8 * freqs), jnp.bfloat16),
            pltpu.VMEM((2 * freqs, 4 * ntime), jnp.bfloat16),
            pltpu.SemaphoreType.DMA((5,)),
        ],
        compiler_params=pltpu.CompilerParams(
            collective_id=0, has_side_effects=True, vmem_limit_bytes=48 * 1024 * 1024
        ),
    )(
        station_index,
        shape_az,
        rates,
        state_in.reshape(runs, span_az, radii),
        chunks(base_flow, base_rows),
        forcing_in.reshape(runs, span_az, radii),
        jnp.asarray(omegas),
        right_table(inverse_p.T),
        right_table(slopes.T),
        left_table(inverse.transpose(2, 0, 1).reshape(ntime, 2 * freqs)),
        left_table(forward.reshape(2 * freqs, ntime)),
    )

    return tuple(finish(y, nf, per_dev, variables, own_az, radii, rows, count) for y in outs)


def finish(y, nf, per_dev, variables, own_az, radii, rows, count):
    y = y.reshape(nf, rows, radii)[:, :count].reshape(nf, -1, own_az, radii)
    return y.transpose(1, 0, 2, 3).reshape(2, per_dev, variables, nf * own_az, radii)


MESH = pl.DeviceIdType.MESH


def solution(mesh):
    return jax.shard_map(
        per_device,
        mesh=mesh,
        in_specs=(
            P(None, "freq", None, "plane", None),
            P(None, "freq", None, "plane", None),
            P("freq", None, "plane", None),
            P(),
            P(),
        ),
        out_specs=(P(None, "freq", None, "plane", None), P(None, "freq", None, "plane", None)),
        check_vma=False,
    )
```

```python
import functools
import math

import jax
import jax.numpy as jnp
import numpy as np
from jax import lax
from jax.experimental import pallas as pl
from jax.experimental.pallas import tpu as pltpu
from jax.sharding import PartitionSpec as P

SWEEPS = 4
STEPS = 2


SIDE_WEIGHT = 1.25
MARCH_WEIGHT = 4.0
DIAG_SHIFT = 4.0
ADVECT_SCALE = 0.5
BASE_SCALE = 0.5


def radial_tables(radius_count):
    indices = np.arange(radius_count)
    angles = math.pi * indices / (radius_count - 1)
    nodes = np.cos(angles)
    weights = np.where((indices == 0) | (indices == radius_count - 1), 2.0, 1.0)
    parity = 1.0 - 2.0 * ((indices[:, None] + indices[None, :]) % 2)
    offdiag = indices[:, None] != indices[None, :]
    spacing = np.where(offdiag, nodes[:, None] - nodes[None, :], 1.0)
    entries = np.where(offdiag, weights[:, None] / weights[None, :] * parity / spacing, 0.0)
    entries = entries - np.diag(entries.sum(axis=1))
    slopes = np.sin(angles)[:, None] * entries / (radius_count - 1)
    system = slopes.T @ slopes + DIAG_SHIFT * np.eye(radius_count)
    return slopes.astype(np.float32), np.linalg.inv(system).astype(np.float32)


def transform_tables(mode_ids, freqs, ntime):
    time_ids = np.arange(ntime)
    angles = 2.0 * math.pi * (mode_ids[:, None] * time_ids[None, :] % ntime) / ntime
    stacked = np.stack([np.cos(angles), -np.sin(angles)])
    return (
        (stacked / math.sqrt(freqs)).astype(np.float32),
        (stacked / math.sqrt(ntime)).astype(np.float32),
    )


def chevron(lobe_count, azimuths, start_az, total_az):
    position = start_az + jnp.arange(azimuths)
    phases = lobe_count[0] * position % total_az
    return 1.0 + 0.5 * jnp.cos(2.0 * math.pi * phases.astype(jnp.float32) / total_az)


def halves(x):
    high = x.astype(jnp.bfloat16)
    return high, (x - high.astype(jnp.float32)).astype(jnp.bfloat16)


def right_table(table):
    high, low = np_halves(table)
    return jnp.asarray(np.tile(np.concatenate([high, low], axis=1), (2, 1)))


def left_table(table):
    high, low = np_halves(table)
    return jnp.asarray(np.concatenate([high, high, low, low], axis=1))


def np_halves(table):
    high = table.astype(jnp.bfloat16)
    return high, (table - high.astype(np.float32)).astype(jnp.bfloat16)


def times_right(x, table):
    width = table.shape[1] // 2
    y = jnp.dot(jnp.concatenate(halves(x), axis=1), table, preferred_element_type=jnp.float32)
    return y[:, :width] + y[:, width:]


def times_left(table, x):
    high, low = halves(x)
    return jnp.dot(
        table,
        jnp.concatenate([high, low, high, low], axis=0),
        preferred_element_type=jnp.float32,
    )


def ring_of(f, p, nf, planes):
    at = f
    if nf % 4 == 0:
        high = nf // 4
        z, y, x = f // 4, (f // 2) % 2, f % 2
        column = 2 * y + (x + y) % 2
        at = column * high + z + (column % 2) * (high - 1 - 2 * z)
    return at * planes + p


def device_of(g, nf, planes):
    at = g // planes
    f = at
    if nf % 4 == 0:
        high = nf // 4
        column, z = at // high, at % high
        z = z + (column % 2) * (high - 1 - 2 * z)
        y = column // 2
        f = 4 * z + 2 * y + (column + y) % 2
    return f, g % planes


def march(
    dims,
    station_ref,
    shape_ref,
    rate_ref,
    state_ref,
    s_base,
    forcing_ref,
    far_omega,
    far_qt,
    far_st,
    far_inv,
    far_fwd,
    g_state,
    g_forcing,
    r_state,
    r_base,
    s_state,
    s_w,
    r_w,
    plane_w,
    x_one,
    b_one,
    edge_out,
    edge_in,
    x_ref,
    b_ref,
    f_ref,
    w_ref,
    o_state,
    o_forcing,
    send_sem,
    recv_sem,
    own_sem,
    halo_send,
    halo_recv,
    edge_send,
    edge_recv,
    load_sem,
    omega_ref,
    qt_ref,
    st_ref,
    inv_ref,
    fwd_ref,
    table_sem,
):
    nf, planes, own_az, variables, per_dev, radii, stored, rows, base_rows, w_rows = dims
    freqs = nf * per_dev
    span = nf * own_az
    runs = 2 * per_dev * variables
    ntime = inv_ref.shape[0]
    half = variables * freqs
    me = lax.axis_index("freq")
    plane = lax.axis_index("plane")
    ring = nf * planes
    here = ring_of(me, plane, nf, planes)
    part, block = here // nf, here % nf

    def named(device):
        return {"freq": device[0], "plane": device[1]}

    right_id = named(device_of((here + 1) % ring, nf, planes))
    left_id = named(device_of((here + ring - 1) % ring, nf, planes))
    barrier = pltpu.get_barrier_semaphore()

    @pl.loop(1, ring)
    def _(d):
        other = (me * planes + plane + d) % ring
        pl.semaphore_signal(
            barrier,
            inc=1,
            device_id={"freq": other // planes, "plane": other % planes},
            device_id_type=MESH,
        )

    beyond = {"freq": me, "plane": (plane + 1) % planes}
    behind = {"freq": me, "plane": (plane + planes - 1) % planes}
    load_state = pltpu.make_async_copy(state_ref, x_one.at[0, :, pl.ds(8, span), :], load_sem.at[0])
    load_forcing = pltpu.make_async_copy(forcing_ref, b_one, load_sem.at[1])
    load_state.start()
    load_forcing.start()
    tables = [
        pltpu.make_async_copy(far, near, table_sem.at[i])
        for i, (far, near) in enumerate(
            (
                (far_omega, omega_ref),
                (far_qt, qt_ref),
                (far_st, st_ref),
                (far_inv, inv_ref),
                (far_fwd, fwd_ref),
            )
        )
    ]
    for table in tables:
        table.start()
    pl.semaphore_wait(barrier, ring - 1)

    def owner(i):
        return device_of(plane * nf + i, nf, planes)

    def holder(i):
        return i, part

    def is_me(device):
        return (device[0] == me) & (device[1] == plane)

    def exchange(k, source, landing, target, origin, pick, mine, size, first):
        def rows_of(ref, i):
            return ref.at[pl.ds(pl.multiple_of(i * size, 8), size), :]

        def copy(i):
            return pltpu.make_async_remote_copy(
                src_ref=rows_of(source, pick(i)),
                dst_ref=rows_of(landing, mine),
                send_sem=send_sem.at[k, i],
                recv_sem=recv_sem.at[k, mine],
                device_id=named(target(i)),
                device_id_type=MESH,
            )

        def arrival(i):
            return pltpu.make_async_remote_copy(
                src_ref=rows_of(landing, i),
                dst_ref=rows_of(landing, i),
                send_sem=send_sem.at[k, i],
                recv_sem=recv_sem.at[k, i],
                device_id=named(origin(i)),
                device_id_type=MESH,
            )

        def own(i):
            return pltpu.make_async_copy(
                rows_of(source, pick(i)), rows_of(landing, mine), own_sem.at[k]
            )

        @pl.loop(0, nf)
        def _(d):
            i = (d + me) % nf
            stays = is_me(target(i))

            @pl.when(stays)
            def _():
                if first:
                    own(i).start()
                else:
                    own(i).wait()

            @pl.when(jnp.logical_not(stays))
            def _():
                if first:
                    copy(i).start()
                else:
                    copy(i).wait_send()

            if not first:

                @pl.when(jnp.logical_not(is_me(origin(i))))
                def _():
                    arrival(i).wait_recv()

    def same(i):
        return i

    base_args = (1, s_base, r_base, owner, holder, same, me, base_rows)
    state_args = (0, s_state, r_state, owner, holder, same, me, rows)
    w_args = (2, s_w, r_w, holder, owner, lambda i: 0, block, w_rows)
    out_state_args = (3, o_state, g_state, holder, owner, same, block, rows)
    out_forcing_args = (4, o_forcing, g_forcing, holder, owner, same, block, rows)
    exchange(*base_args, True)

    def halo_copies(e):
        slot = e % 2
        return (
            pltpu.make_async_remote_copy(
                src_ref=x_ref.at[slot, own_az],
                dst_ref=x_ref.at[slot, 0],
                send_sem=halo_send.at[0, e],
                recv_sem=halo_recv.at[0, e],
                device_id=right_id,
                device_id_type=MESH,
            ),
            pltpu.make_async_remote_copy(
                src_ref=x_ref.at[slot, 1],
                dst_ref=x_ref.at[slot, own_az + 1],
                send_sem=halo_send.at[1, e],
                recv_sem=halo_recv.at[1, e],
                device_id=left_id,
                device_id_type=MESH,
            ),
        )

    def place(a, c, v, kk):
        return ((c * variables + v) * per_dev + kk) * nf

    def packed_row(a, c, v, kk):
        return ((c * per_dev + kk) * variables + v) * own_az + a

    def each_run(visit):
        @pl.loop(0, own_az)
        def _(a):
            for c in range(2):
                for v in range(variables):
                    for kk in range(per_dev):
                        visit(a, place(a, c, v, kk), packed_row(a, c, v, kk))

    def in_row(a, c, v, kk):
        return ((c * per_dev + kk) * variables + v) * own_az + a

    def edge_copies(e):
        return [
            pltpu.make_async_remote_copy(
                src_ref=edge_out.at[e, side],
                dst_ref=edge_in.at[e, side],
                send_sem=edge_send.at[side, e],
                recv_sem=edge_recv.at[side, e],
                device_id=target,
                device_id_type=MESH,
            )
            for side, target in ((0, beyond), (1, behind))
        ]

    def send_edges(slot, e):
        for m in range(runs):
            edge_out[e, 0, pl.ds(m, 1), :] = x_one[slot, m, pl.ds(7 + span, 1), :]
            edge_out[e, 1, pl.ds(m, 1), :] = x_one[slot, m, pl.ds(8, 1), :]
        for copy in edge_copies(e):
            copy.start()

    for table in tables:
        table.wait()
    load_state.wait()
    send_edges(0, 0)
    load_forcing.wait()

    @pl.loop(0, runs)
    def _(m):
        b_one[m] = MARCH_WEIGHT * x_one[0, m, pl.ds(8, span), :] + b_one[m]

    exchange(*base_args, False)
    for station in range(STEPS):
        wanted = station_ref[station]

        @pl.loop(0, own_az)
        def _(a):
            for v in range(variables):
                scaled = (BASE_SCALE * shape_ref[a]) * r_base[
                    pl.ds(
                        (wanted // stored) * base_rows
                        + ((wanted % stored) * variables + v) * own_az
                        + a,
                        1,
                    ),
                    :,
                ]
                if station == 0:
                    s_w[pl.ds(v * own_az + a, 1), :] = scaled
                else:
                    w_ref[(station - 1) * own_az + a, pl.ds(v, 1), :] = scaled

        if station == 0:
            exchange(*w_args, True)
    exchange(*w_args, False)

    @pl.loop(0, nf)
    def _(j):
        for v in range(variables):
            plane_w[v, pl.ds(j * own_az, own_az), :] = r_w[pl.ds(j * w_rows + v * own_az, own_az), :]

    @pl.loop(0, SWEEPS)
    def _(e):
        src, dst = e % 2, (e + 1) % 2
        for copy in edge_copies(e):
            copy.wait()
        for m in range(runs):
            x_one[src, m, pl.ds(7, 1), :] = edge_in[e, 0, pl.ds(m, 1), :]
            x_one[src, m, pl.ds(8 + span, 1), :] = edge_in[e, 1, pl.ds(m, 1), :]
        for kk in range(per_dev):
            rate = rate_ref[kk]

            @pl.loop(0, variables)
            def _(v):
                w = plane_w[v]
                at = [(c * per_dev + kk) * variables + v for c in range(2)]
                real, imag = [x_one[src, m, pl.ds(8, span), :] for m in at]
                mixing = (w * real - rate * imag, w * imag + rate * real)
                summed = [
                    SIDE_WEIGHT
                    * (x_one[src, m, pl.ds(7, span), :] + x_one[src, m, pl.ds(9, span), :])
                    + b_one[m]
                    - mixed
                    for m, mixed in zip(at, mixing)
                ]
                q = times_right(jnp.concatenate(summed, axis=0), qt_ref[...])
                x_one[dst, at[0], pl.ds(8, span), :] = q[:span]
                x_one[dst, at[1], pl.ds(8, span), :] = q[span:]

        @pl.when(e < SWEEPS - 1)
        def _():
            send_edges(dst, e + 1)

    settled = SWEEPS % 2

    @pl.loop(0, nf)
    def _(j):
        for m in range(runs):
            s_state[pl.ds(j * rows + m * own_az, own_az), :] = x_one[
                settled, m, pl.ds(8 + j * own_az, own_az), :
            ]

    exchange(*state_args, True)
    exchange(*state_args, False)

    def unpack_state(a, start, row):
        x_ref[0, a + 1, pl.ds(start, nf), :] = r_state[pl.ds(row, nf, stride=rows), :]

    each_run(unpack_state)
    for copy in halo_copies(0):
        copy.start()
    omega = omega_ref[...][None]
    flat = (2 * half, radii)
    cube = (variables, freqs, radii)

    def sweep_slab(src, dst, a, station):
        x = x_ref[src, a + 1]
        beside = SIDE_WEIGHT * (x_ref[src, a] + x_ref[src, a + 2]) + b_ref[a]
        real, imag = x[:half].reshape(cube), x[half:].reshape(cube)
        w = w_ref[(station - 1) * own_az + a][:variables][:, None, :]
        mixing = jnp.concatenate([w * real - omega * imag, w * imag + omega * real], axis=0)
        summed = beside - mixing.reshape(flat)
        x_ref[dst, a + 1] = times_right(summed, qt_ref[...])

    def advect_slab(slot, a, final):
        x = x_ref[slot, a + 1]
        beside = 0.5 * (x_ref[slot, a + 2] - x_ref[slot, a])

        def lanes(y):
            return [
                jnp.concatenate(
                    [
                        y[v * freqs : (v + 1) * freqs],
                        y[half + v * freqs : half + (v + 1) * freqs],
                    ],
                    axis=0,
                )
                for v in range(variables)
            ]

        both = jnp.concatenate(lanes(x) + lanes(beside), axis=1)
        in_time = times_left(inv_ref[...], both)
        u = [in_time[:, v * radii : (v + 1) * radii] for v in range(variables)]
        ua = [
            in_time[:, (variables + v) * radii : (variables + v + 1) * radii]
            for v in range(variables)
        ]
        radial = times_right(jnp.concatenate(u, axis=0), st_ref[...])
        ur = [radial[v * ntime : (v + 1) * ntime] for v in range(variables)]
        n = [u[1] * ur[v] + u[2] * ua[v] for v in range(variables)]
        n[0] = n[0] + u[0] * (ur[1] + ua[2])
        source = -ADVECT_SCALE * jnp.concatenate(n, axis=1)
        spectral = times_left(fwd_ref[...], source)
        forcing = jnp.concatenate(
            [
                spectral[c * freqs : (c + 1) * freqs, v * radii : (v + 1) * radii]
                for c in range(2)
                for v in range(variables)
            ],
            axis=0,
        )
        if final:
            f_ref[a] = forcing
        else:
            b_ref[a] = MARCH_WEIGHT * x + forcing

    def advect_all(slot, e, final):
        @pl.loop(1, own_az - 1)
        def _(a):
            advect_slab(slot, a, final)

        for copy in halo_copies(e):
            copy.wait()
        advect_slab(slot, 0, final)
        if own_az > 1:
            advect_slab(slot, own_az - 1, final)

    advect_all(0, 0, False)
    for station in range(1, STEPS):

        @pl.loop(0, SWEEPS)
        def _(sweep):
            e = (station - 1) * SWEEPS + sweep
            src, dst = e % 2, (e + 1) % 2

            @pl.when(sweep > 0)
            def _():
                for copy in halo_copies(e):
                    copy.wait()

            sweep_slab(src, dst, 0, station)
            if own_az > 1:
                sweep_slab(src, dst, own_az - 1, station)
            for copy in halo_copies(e + 1):
                copy.start()

            @pl.loop(1, own_az - 1)
            def _(a):
                sweep_slab(src, dst, a, station)

        last = station * SWEEPS
        slot = last % 2
        final = station == STEPS - 1
        if final:

            def pack_state(a, start, row):
                o_state[pl.ds(row, nf, stride=rows), :] = x_ref[slot, a + 1, pl.ds(start, nf), :]

            each_run(pack_state)
            exchange(*out_state_args, True)

        advect_all(slot, last, final)

    def pack_forcing(a, start, row):
        o_forcing[pl.ds(row, nf, stride=rows), :] = f_ref[a, pl.ds(start, nf), :]

    each_run(pack_forcing)
    exchange(*out_forcing_args, True)
    exchange(*out_state_args, False)
    exchange(*out_forcing_args, False)


def per_device(state_in, forcing_in, base_flow, station_index, lobe_count):
    _, per_dev, variables, span_az, radii = state_in.shape
    nf = lax.axis_size("freq")
    planes = lax.axis_size("plane")
    freqs = per_dev * nf
    ntime = 3 * freqs // 2
    own_az = span_az // nf
    stored = base_flow.shape[0]
    slopes, inverse_p = radial_tables(radii)
    mode_ids = (np.arange(nf)[None, :] * per_dev + np.arange(per_dev)[:, None]).reshape(-1)
    inverse, forward = transform_tables(mode_ids, freqs, ntime)
    omegas = np.broadcast_to((0.5 * mode_ids / freqs).astype(np.float32)[:, None], (freqs, radii))
    plane = lax.axis_index("plane")
    here = ring_of(lax.axis_index("freq"), plane, nf, planes)
    shape_az = chevron(lobe_count, own_az, here * own_az, span_az * planes)

    def padded_rows(count):
        return -(-count // 8) * 8

    def chunks(x, size):
        x = x.reshape(-1, nf, own_az, radii).transpose(1, 0, 2, 3).reshape(nf, -1, radii)
        x = jnp.pad(x, ((0, 0), (0, size - x.shape[1]), (0, 0)))
        return x.reshape(nf * size, radii)

    count = 2 * per_dev * variables * own_az
    rows = padded_rows(count)
    base_rows = padded_rows(stored * variables * own_az)
    w_rows = padded_rows(variables * own_az)
    dims = (nf, planes, own_az, variables, per_dev, radii, stored, rows, base_rows, w_rows)
    half = variables * freqs
    exchanges = (STEPS - 1) * SWEEPS + 1
    runs = 2 * per_dev * variables
    edge_rows = padded_rows(runs)
    first_mode = lax.axis_index("freq") * per_dev
    rates = 0.5 * (first_mode + jnp.arange(per_dev)).astype(jnp.float32) / freqs
    smem = pl.BlockSpec(memory_space=pltpu.SMEM)
    anywhere = pl.BlockSpec(memory_space=pl.ANY)
    packed = (nf * rows, radii)
    f32 = jnp.float32
    outs = pl.pallas_call(
        functools.partial(march, dims),
        out_shape=[jax.ShapeDtypeStruct(packed, f32)] * 2,
        in_specs=[smem, smem, smem, anywhere, anywhere, anywhere] + [anywhere] * 5,
        out_specs=[anywhere, anywhere],
        scratch_shapes=[
            pltpu.VMEM(packed, f32),
            pltpu.VMEM((nf * base_rows, radii), f32),
            pltpu.VMEM(packed, f32),
            pltpu.VMEM((w_rows, radii), f32),
            pltpu.VMEM((nf * w_rows, radii), f32),
            pltpu.VMEM((variables, span_az, radii), f32),
            pltpu.VMEM((2, runs, span_az + 16, radii), f32),
            pltpu.VMEM((runs, span_az, radii), f32),
            pltpu.VMEM((SWEEPS, 2, edge_rows, radii), f32),
            pltpu.VMEM((SWEEPS, 2, edge_rows, radii), f32),
            pltpu.VMEM((2, own_az + 2, 2 * half, radii), f32),
            pltpu.VMEM((own_az, 2 * half, radii), f32),
            pltpu.VMEM((own_az, 2 * half, radii), f32),
            pltpu.VMEM(((STEPS - 1) * own_az, padded_rows(variables), radii), f32),
            pltpu.VMEM(packed, f32),
            pltpu.VMEM(packed, f32),
            pltpu.SemaphoreType.DMA((5, nf)),
            pltpu.SemaphoreType.DMA((5, nf)),
            pltpu.SemaphoreType.DMA((5,)),
            pltpu.SemaphoreType.DMA((2, exchanges)),
            pltpu.SemaphoreType.DMA((2, exchanges)),
            pltpu.SemaphoreType.DMA((2, SWEEPS)),
            pltpu.SemaphoreType.DMA((2, SWEEPS)),
            pltpu.SemaphoreType.DMA((2,)),
            pltpu.VMEM((freqs, radii), f32),
            pltpu.VMEM((2 * radii, 2 * radii), jnp.bfloat16),
            pltpu.VMEM((2 * radii, 2 * radii), jnp.bfloat16),
            pltpu.VMEM((ntime, 8 * freqs), jnp.bfloat16),
            pltpu.VMEM((2 * freqs, 4 * ntime), jnp.bfloat16),
            pltpu.SemaphoreType.DMA((5,)),
        ],
        compiler_params=pltpu.CompilerParams(
            collective_id=0, has_side_effects=True, vmem_limit_bytes=63_000 * 1024
        ),
    )(
        station_index,
        shape_az,
        rates,
        state_in.reshape(runs, span_az, radii),
        chunks(base_flow, base_rows),
        forcing_in.reshape(runs, span_az, radii),
        jnp.asarray(omegas),
        right_table(inverse_p.T),
        right_table(slopes.T),
        left_table(inverse.transpose(2, 0, 1).reshape(ntime, 2 * freqs)),
        left_table(forward.reshape(2 * freqs, ntime)),
    )

    return tuple(finish(y, nf, per_dev, variables, own_az, radii, rows, count) for y in outs)


def finish(y, nf, per_dev, variables, own_az, radii, rows, count):
    y = y.reshape(nf, rows, radii)[:, :count].reshape(nf, -1, own_az, radii)
    return y.transpose(1, 0, 2, 3).reshape(2, per_dev, variables, nf * own_az, radii)


MESH = pl.DeviceIdType.MESH


def solution(mesh):
    return jax.shard_map(
        per_device,
        mesh=mesh,
        in_specs=(
            P(None, "freq", None, "plane", None),
            P(None, "freq", None, "plane", None),
            P("freq", None, "plane", None),
            P(),
            P(),
        ),
        out_specs=(P(None, "freq", None, "plane", None), P(None, "freq", None, "plane", None)),
        check_vma=False,
    )
```
